32 devices in a mesh: groups: 2 (over x), dp: 8 (over z, y), expert: 2 (over core).
Axes of the slice: x: 2, y: 2, z: 4, core: 2. Of those that a mesh axis runs over, the one named last changes fastest.
Arguments:
- tokens: bfloat16 [128, 4096], P(('groups', 'dp', 'expert')), parts along dimension 0, may hold values from -6 to 6
- cotangent: bfloat16 [128, 4096], P(('groups', 'dp', 'expert')), parts along dimension 0, may hold values from -6 to 6
- routing: int32 [128, 2], P(('groups', 'dp', 'expert')), parts along dimension 0, may hold values from 0 to 7, as said below
- gate_first: int32 [128], P(('groups', 'dp', 'expert')), parts along dimension 0, may hold values from 1 to 1023
- gate_weight: bfloat16 [4096, 65536], P(None, ('dp', 'expert')), may hold values from -0.09375 to 0.09375
- up_weight: bfloat16 [4096, 65536], P(None, ('dp', 'expert')), may hold values from -0.09375 to 0.09375
- down_weight: bfloat16 [65536, 4096], P(('dp', 'expert')), may hold values from -0.0625 to 0.0625
Outputs:
- mixed: bfloat16 [128, 4096], P(('groups', 'dp', 'expert')), parts along dimension 0
- token_grad: bfloat16 [128, 4096], P(('groups', 'dp', 'expert')), parts along dimension 0
- gate_grad: float32 [128, 2], P(('groups', 'dp', 'expert')), parts along dimension 0
The draws below stay inside these ranges and needn't reach their ends.
There are 2 independent parts, one for each index of `groups`. The reference program is written for one: setup_inputs(seed, part) draws one part's arguments, and reference() takes and returns one part's arrays. A program takes and returns all parts, laid end to end along the dimension named above; an argument that names none is the same for every part. Nothing has to cross between parts.
Inputs may be any that keep to these rules, and one draw needn't show every extreme that they name: `routing`: the two experts of a token differ. Among the 4 tokens of one device (aligned blocks of 4 rows) no expert is named more than 2 times, and one expert is named exactly 2 times in every such block.
All inputs are finite; a program needn't handle non-finite values.
Results may differ from the reference program's by a relative error of at most 0.014.
Values may be sent and summed in bfloat16 or wider, within the bound.
A program may use at most 192 MiB of HBM per device.

```python
import jax
import jax.numpy as jnp
from jax import lax

D = 4096
E = 8
FF_WIN = 8192
TOK_DEV = 4
CAP = 2
TOKENS = 64
N_DP = 8
N_EXPERT = 2


def permute_rows(block_keys, length):

    def permute_one(one_key):
        return jax.random.permutation(one_key, length)
    return jax.vmap(permute_one)(block_keys)


def draw_routing(key, part):
    key_hot, key_order, key_shift, key_rows, key_swap = jax.random.split(key, 5)
    block_count = TOKENS // TOK_DEV
    hot_expert = jax.random.randint(key_hot, (), 0, E)
    others = permute_rows(jax.random.split(key_order, block_count), E - 1).astype(jnp.int32)
    others = (hot_expert + 1 + others) % E
    shift = jax.random.randint(key_shift, (block_count, 1), 0, CAP)
    positions = jnp.arange(2 * TOK_DEV, dtype=jnp.int32)[None, :]
    run_index = jnp.clip((positions - CAP + shift) // CAP, 0, E - 2)
    run_index = jnp.broadcast_to(run_index, (block_count, 2 * TOK_DEV))
    other_pick = jnp.take_along_axis(others, run_index, axis=1)
    listed = jnp.where(positions < CAP, hot_expert, other_pick)
    first_col = listed[:, :TOK_DEV]
    second_col = listed[:, TOK_DEV:]
    swap_bits = jax.random.randint(key_swap, (block_count, TOK_DEV), 0, 2)
    col_left = jnp.where(swap_bits == 1, second_col, first_col)
    col_right = jnp.where(swap_bits == 1, first_col, second_col)
    row_order = permute_rows(jax.random.split(key_rows, block_count), TOK_DEV).astype(jnp.int32)
    inverse = jnp.argsort(row_order, axis=1)
    col_left = jnp.take_along_axis(col_left, inverse, axis=1)
    col_right = jnp.take_along_axis(col_right, inverse, axis=1)
    return jnp.stack([col_left, col_right], axis=-1).reshape(TOKENS, 2).astype(jnp.int32)


def set_ends(result, own_key, low, top_value):
    shape = result.shape
    place = [jax.random.randint(jax.random.fold_in(own_key, axis), (), 0, shape[axis]) for axis in range(len(shape))]
    result = result.at[tuple(place)].set(low)
    longest = shape.index(max(shape))
    place[longest] = (place[longest] + 1) % shape[longest]
    return result.at[tuple(place)].set(top_value)


def level_of(rng, dims, pieces, least, high):
    loudness, own = 1.0, jax.random.fold_in(rng, 6)
    for dim, shards_of in pieces:
        heights = jnp.exp(jax.random.uniform(jax.random.fold_in(own, dim), (shards_of,), jnp.float32, least / len(pieces), high / len(pieces)))
        loudness = loudness * jnp.repeat(heights, dims[dim] // shards_of).reshape([-1 if axis == dim else 1 for axis in range(len(dims))])
    return loudness


def gaussian(stream_key, shape, deviation, limit, cuts=(), held_as=jnp.bfloat16):
    values = deviation * jax.random.normal(stream_key, shape, jnp.float32)
    if cuts:
        values = values * level_of(stream_key, shape, cuts, -0.22, 0.18)
    return jnp.clip(values, -limit, limit).astype(held_as)


def setup_inputs(seed: int = 0, part: int = 0) -> dict:
    arg_keys = jax.random.split(jax.random.key(seed), 8)
    part_keys = jax.random.split(jax.random.fold_in(arg_keys[7], part), 8)
    return {
        "tokens": gaussian(part_keys[0], (TOKENS, D), 1.0, 6.0, ((0, 16),)),
        "cotangent": gaussian(part_keys[1], (TOKENS, D), 1.0, 6.0, ((0, 16),)),
        "routing": draw_routing(jax.random.fold_in(jax.random.fold_in(arg_keys[7], part), 71), part),
        "gate_first": set_ends(jax.random.randint(part_keys[3], (TOKENS,), 1, 1024), jax.random.fold_in(part_keys[3], 1), 1, 1023).astype(jnp.int32),
        "gate_weight": gaussian(arg_keys[4], (D, E * FF_WIN), D ** -0.5, 0.09375, ((1, 16),)),
        "up_weight": gaussian(arg_keys[5], (D, E * FF_WIN), D ** -0.5, 0.09375, ((1, 16),)),
        "down_weight": gaussian(arg_keys[6], (E * FF_WIN, D), FF_WIN ** -0.5, 0.0625, ((0, 16),)),
    }


def block_sum(left, right_blocks):
    group_count = right_blocks.shape[0]
    block_width = right_blocks.shape[1]
    rows_here = left.shape[0]
    split_left = left.reshape(rows_here, group_count, block_width).astype(jnp.float32)
    terms = jnp.einsum("rgh,ghd->grd", split_left, right_blocks.astype(jnp.float32))
    return terms


def round_sum(terms):
    rounded = lax.optimization_barrier(terms.astype(jnp.bfloat16))
    return jnp.sum(rounded.astype(jnp.float32), axis=0)


def reference(tokens, cotangent, routing, gate_first, gate_weight, up_weight, down_weight):
    share_first = gate_first.astype(jnp.float32) / 1024.0
    share_second = (1024 - gate_first).astype(jnp.float32) / 1024.0
    most_rows = (TOKENS // TOK_DEV) * CAP
    group_count = (N_DP * N_EXPERT) // E
    block_width = FF_WIN // group_count

    def one_expert(carry, expert_id):
        mixed_sum, grad_sum, score_sum = carry
        in_first = routing[:, 0] == expert_id
        in_second = routing[:, 1] == expert_id
        chosen = in_first | in_second
        weight_all = jnp.where(in_first, share_first, 0.0) + jnp.where(in_second, share_second, 0.0)
        row_ids = jnp.nonzero(chosen, size=most_rows, fill_value=0)[0].astype(jnp.int32)
        live_rows = jnp.arange(most_rows, dtype=jnp.int32) < jnp.sum(chosen.astype(jnp.int32))
        row_weight = jnp.where(live_rows, weight_all[row_ids], 0.0)
        inputs = tokens[row_ids]
        grads_in = cotangent[row_ids]
        start = (expert_id * FF_WIN).astype(jnp.int32)
        w_gate = lax.dynamic_slice_in_dim(gate_weight, start, FF_WIN, 1)
        w_up = lax.dynamic_slice_in_dim(up_weight, start, FF_WIN, 1)
        w_down = lax.dynamic_slice_in_dim(down_weight, start, FF_WIN, 0)
        gate_pre = jnp.dot(inputs, w_gate, preferred_element_type=jnp.float32)
        up_pre = jnp.dot(inputs, w_up, preferred_element_type=jnp.float32)
        hidden = (jax.nn.silu(gate_pre) * up_pre).astype(jnp.bfloat16)
        expert_out = round_sum(block_sum(hidden, w_down.reshape(group_count, block_width, D)))
        score = jnp.sum(grads_in.astype(jnp.float32) * expert_out, axis=1)
        score = jnp.where(live_rows, score, 0.0)
        d_hidden = row_weight[:, None] * jnp.dot(grads_in, w_down.T, preferred_element_type=jnp.float32)
        sig_gate = jax.nn.sigmoid(gate_pre)
        d_gate = (d_hidden * up_pre * sig_gate * (1.0 + gate_pre * (1.0 - sig_gate))).astype(jnp.bfloat16)
        d_up = (d_hidden * jax.nn.silu(gate_pre)).astype(jnp.bfloat16)
        grad_terms = block_sum(d_gate, w_gate.T.reshape(group_count, block_width, D))
        grad_terms = grad_terms + block_sum(d_up, w_up.T.reshape(group_count, block_width, D))
        grad_rows = round_sum(grad_terms)
        mixed_sum = mixed_sum.at[row_ids].add(row_weight[:, None] * expert_out)
        grad_sum = grad_sum.at[row_ids].add(jnp.where(live_rows[:, None], grad_rows, 0.0))
        score_full = jnp.zeros((TOKENS,), jnp.float32).at[row_ids].add(score)
        score_sum = score_sum + jnp.stack([jnp.where(in_first, score_full, 0.0), jnp.where(in_second, score_full, 0.0)], axis=1)
        return (mixed_sum, grad_sum, score_sum), None

    start_carry = (jnp.zeros((TOKENS, D), jnp.float32), jnp.zeros((TOKENS, D), jnp.float32), jnp.zeros((TOKENS, 2), jnp.float32))
    final, _ = lax.scan(one_expert, start_carry, jnp.arange(E, dtype=jnp.int32))
    mixed_sum, grad_sum, score_sum = final
    return mixed_sum.astype(jnp.bfloat16), grad_sum.astype(jnp.bfloat16), score_sum
```

```python
import functools

import jax
import jax.numpy as jnp
from jax import lax
from jax.experimental import pallas as pl
from jax.experimental.pallas import tpu as pltpu
from jax.sharding import PartitionSpec as P

E = 8
BLOCK = 256
DEPTH = 7
NN = (((1,), (0,)), ((), ()))
NT = (((1,), (1,)), ((), ()))


def expert_rows(got_x, got_dy, got_w, gate_weight, up_weight, down_weight):
    gate_pre = jnp.dot(got_x, gate_weight, preferred_element_type=jnp.float32)
    up_pre = jnp.dot(got_x, up_weight, preferred_element_type=jnp.float32)
    sig_gate = jax.nn.sigmoid(gate_pre)
    silu_gate = gate_pre * sig_gate
    hidden = (silu_gate * up_pre).astype(jnp.bfloat16)
    part_out = jnp.dot(hidden, down_weight, preferred_element_type=jnp.float32)
    d_hidden = got_w[:, None] * jnp.dot(got_dy, down_weight.T, preferred_element_type=jnp.float32)
    d_gate = (d_hidden * up_pre * sig_gate * (1.0 + gate_pre * (1.0 - sig_gate))).astype(
        jnp.bfloat16
    )
    d_up = (d_hidden * silu_gate).astype(jnp.bfloat16)
    part_grad = jnp.dot(d_gate, gate_weight.T, preferred_element_type=jnp.float32)
    part_grad = part_grad + jnp.dot(d_up, up_weight.T, preferred_element_type=jnp.float32)
    return (part_out.astype(jnp.bfloat16), part_grad.astype(jnp.bfloat16))


def on_device(tokens, cotangent, routing, gate_first, gate_weight, up_weight, down_weight):
    devices = lax.axis_size(("dp", "expert"))
    group_size = devices // E
    tok_rows = tokens.shape[0]
    width = tokens.shape[1]
    capacity = tok_rows // 2
    expert_ids = jnp.arange(E, dtype=jnp.int32)
    first_hot = (routing[:, 0:1] == expert_ids[None, :]).astype(jnp.int32)
    second_hot = (routing[:, 1:2] == expert_ids[None, :]).astype(jnp.int32)
    rank_rows = jnp.cumsum(first_hot + second_hot, axis=0) - 1
    slot_ids = jnp.arange(capacity, dtype=jnp.int32)
    slot_hot = (rank_rows[:, :, None] == slot_ids[None, None, :]).astype(jnp.float32)
    pick_first = first_hot[:, :, None].astype(jnp.float32) * slot_hot
    pick_second = second_hot[:, :, None].astype(jnp.float32) * slot_hot
    picked = pick_first + pick_second
    share_first = gate_first.astype(jnp.float32) / 1024.0
    share_second = (1024 - gate_first).astype(jnp.float32) / 1024.0
    picked_low = picked.astype(jnp.bfloat16)
    send_x = jnp.einsum(
        "tec,td->ecd", picked_low, tokens, preferred_element_type=jnp.float32
    ).astype(jnp.bfloat16)
    send_dy = jnp.einsum(
        "tec,td->ecd", picked_low, cotangent, preferred_element_type=jnp.float32
    ).astype(jnp.bfloat16)
    weighted = pick_first * share_first[:, None, None] + pick_second * share_second[:, None, None]
    send_w = jnp.sum(weighted, axis=0)
    out_x = jnp.repeat(send_x, group_size, axis=0)
    out_dy = jnp.repeat(send_dy, group_size, axis=0)
    out_w = jnp.repeat(send_w, group_size, axis=0)

    def exchange(value):
        return lax.all_to_all(value, ("dp", "expert"), split_axis=0, concat_axis=0, tiled=True)

    recv_x, recv_dy = exchange(out_x), exchange(out_dy)
    recv_w = exchange(out_w.astype(jnp.bfloat16)).astype(out_w.dtype)
    got_x = recv_x.reshape(devices * capacity, width)
    got_dy = recv_dy.reshape(devices * capacity, width)
    got_w = recv_w.reshape(devices * capacity)
    part_out, part_grad = expert_rows(got_x, got_dy, got_w, gate_weight, up_weight, down_weight)
    back_out = exchange(part_out.reshape(devices, capacity, width))
    back_grad = exchange(part_grad.reshape(devices, capacity, width))
    summed_out = jnp.sum(
        back_out.astype(jnp.float32).reshape(E, group_size, capacity, width), axis=1
    )
    summed_grad = jnp.sum(
        back_grad.astype(jnp.float32).reshape(E, group_size, capacity, width), axis=1
    )
    rank_first = jnp.take_along_axis(rank_rows, routing[:, 0:1], axis=1)[:, 0]
    rank_second = jnp.take_along_axis(rank_rows, routing[:, 1:2], axis=1)[:, 0]
    slot_first = routing[:, 0] * capacity + rank_first
    slot_second = routing[:, 1] * capacity + rank_second
    flat_out = summed_out.reshape(E * capacity, width)
    flat_grad = summed_grad.reshape(E * capacity, width)
    out_first = jnp.take(flat_out, slot_first, axis=0)
    out_second = jnp.take(flat_out, slot_second, axis=0)
    mixed = (share_first[:, None] * out_first + share_second[:, None] * out_second).astype(
        jnp.bfloat16
    )
    token_grad = (
        jnp.take(flat_grad, slot_first, axis=0) + jnp.take(flat_grad, slot_second, axis=0)
    ).astype(jnp.bfloat16)
    cot_float = cotangent.astype(jnp.float32)
    grad_first = jnp.sum(cot_float * out_first, axis=1)
    grad_second = jnp.sum(cot_float * out_second, axis=1)
    gate_grad = jnp.stack([grad_first, grad_second], axis=1)
    return (mixed, token_grad, gate_grad)


def layer_kernel(
    n_dp,
    route_ref,
    first_ref,
    x_ref,
    dy_ref,
    gate_hbm,
    up_hbm,
    down_hbm,
    mixed_ref,
    grad_ref,
    score_ref,
    gate_buf,
    up_buf,
    down_buf,
    pack,
    recv,
    xs,
    dys,
    acc_out,
    acc_grad,
    pair_send,
    pair_recv,
    back_send,
    back_recv,
    w_sem,
    send_sem,
    recv_sem,
    fsend_sem,
    frecv_sem,
    own_sem,
    pair_sem,
    bsend_sem,
    brecv_sem,
):
    tok, width = x_ref.shape
    cap = tok // 2
    half = n_dp * cap
    hidden = down_hbm.shape[0]
    blocks = hidden // BLOCK
    dp = lax.axis_index("dp")
    core = lax.axis_index("expert")
    other = 1 - core
    f32, bf16 = jnp.float32, jnp.bfloat16

    def weight_copies(step, slot):
        start = pl.multiple_of(step * BLOCK, BLOCK)
        return (
            pltpu.make_async_copy(
                gate_hbm.at[:, pl.ds(start, BLOCK)], gate_buf.at[slot], w_sem.at[0, slot]
            ),
            pltpu.make_async_copy(
                up_hbm.at[:, pl.ds(start, BLOCK)], up_buf.at[slot], w_sem.at[1, slot]
            ),
            pltpu.make_async_copy(
                down_hbm.at[pl.ds(start, BLOCK), :], down_buf.at[slot], w_sem.at[2, slot]
            ),
        )

    def remote(src, dst, send, arrive, q, c):
        return pltpu.make_async_remote_copy(
            src_ref=src,
            dst_ref=dst,
            send_sem=send,
            recv_sem=arrive,
            device_id={"dp": q, "expert": c},
            device_id_type=pl.DeviceIdType.MESH,
        )

    barrier = pltpu.get_barrier_semaphore()
    for k in range(1, n_dp):
        pl.semaphore_signal(
            barrier,
            inc=1,
            device_id={"dp": lax.rem(dp + k, n_dp), "expert": core},
            device_id_type=pl.DeviceIdType.MESH,
        )
    pl.semaphore_signal(
        barrier,
        inc=1,
        device_id={"dp": dp, "expert": other},
        device_id_type=pl.DeviceIdType.MESH,
    )

    ahead = min(DEPTH, blocks)
    for step in range(ahead):
        for copy in weight_copies(step, step):
            copy.start()

    slots = []
    for t in range(tok):
        row = []
        for j in range(2):
            e = route_ref[t, j]
            rank = jnp.int32(0)
            for s in range(t):
                rank = rank + jnp.where((route_ref[s, 0] == e) | (route_ref[s, 1] == e), 1, 0)
            row.append(e * cap + rank)
        slots.append(row)

    slot_rows = lax.broadcasted_iota(jnp.int32, (half, width), 0)
    for which, ref in ((0, x_ref), (1, dy_ref)):
        rows = ref[...].astype(f32)
        packed = jnp.zeros((half, width), f32)
        for t in range(tok):
            chosen = (slot_rows == slots[t][0]) | (slot_rows == slots[t][1])
            packed = jnp.where(chosen, jnp.broadcast_to(rows[t : t + 1, :], (half, width)), packed)
        for e in range(n_dp):
            pack[which, e] = packed[e * cap : (e + 1) * cap, :].astype(bf16)

    pl.semaphore_wait(barrier, n_dp)

    mine = core * n_dp + dp
    sends = []
    for k in range(1, n_dp):
        q = lax.rem(dp + k, n_dp)
        copy = remote(
            pack.at[:, q], recv.at[:, mine], send_sem.at[k], recv_sem.at[k], q, core
        )
        copy.start()
        sends.append(copy)
    own = pltpu.make_async_copy(pack.at[:, dp], recv.at[:, mine], own_sem.at[0])
    own.start()
    forwards = [
        remote(pack.at[:, dp], recv.at[:, mine], fsend_sem.at[0], frecv_sem.at[0], dp, other)
    ]
    forwards[0].start()
    for k in range(1, n_dp):
        slot = core * n_dp + lax.rem(dp + n_dp - k, n_dp)
        sends[k - 1].wait_recv()
        copy = remote(
            recv.at[:, slot], recv.at[:, slot], fsend_sem.at[k], frecv_sem.at[k], dp, other
        )
        copy.start()
        forwards.append(copy)
    own.wait()
    for copy in forwards:
        copy.wait_recv()

    xs[...] = recv[0].astype(f32).reshape(2 * half, width).astype(bf16)
    dys[...] = recv[1].astype(f32).reshape(2 * half, width).astype(bf16)
    acc_out[...] = jnp.zeros_like(acc_out)
    acc_grad[...] = jnp.zeros_like(acc_grad)

    @pl.loop(0, blocks)
    def _(step):
        slot = lax.rem(step, ahead)
        for copy in weight_copies(step, slot):
            copy.wait()
        w_gate, w_up, w_down = gate_buf.at[slot], up_buf.at[slot], down_buf.at[slot]
        gate_pre = lax.dot_general(xs[...], w_gate[...], NN, preferred_element_type=f32)
        up_pre = lax.dot_general(xs[...], w_up[...], NN, preferred_element_type=f32)
        d_hidden = lax.dot_general(dys[...], w_down[...], NT, preferred_element_type=f32)
        sig = 1.0 / (1.0 + jnp.exp(-gate_pre))
        silu = gate_pre * sig
        hid = (silu * up_pre).astype(bf16)
        d_gate = (d_hidden * up_pre * sig * (1.0 + gate_pre * (1.0 - sig))).astype(bf16)
        d_up = (d_hidden * silu).astype(bf16)
        acc_out[...] += lax.dot_general(hid, w_down[...], NN, preferred_element_type=f32)
        acc_grad[...] += lax.dot_general(
            d_gate, w_gate[...], NT, preferred_element_type=f32
        ) + lax.dot_general(d_up, w_up[...], NT, preferred_element_type=f32)

        @pl.when(step + ahead < blocks)
        def _():
            for copy in weight_copies(step + ahead, slot):
                copy.start()

    for copy in sends:
        copy.wait_send()
    for copy in forwards:
        copy.wait_send()

    keep = pl.ds(pl.multiple_of(core * half, half), half)
    give = pl.ds(pl.multiple_of(other * half, half), half)
    pair_send[0] = acc_out[give, :].astype(bf16)
    pair_send[1] = acc_grad[give, :].astype(bf16)
    pair = remote(pair_send, pair_recv, pair_sem.at[0], pair_sem.at[1], dp, other)
    pair.start()
    pair.wait()
    for which, acc in ((0, acc_out), (1, acc_grad)):
        total = acc[keep, :] + pair_recv[which].astype(f32)
        for q in range(n_dp):
            back_send[q, which] = total[q * cap : (q + 1) * cap, :].astype(bf16)
    backs = []
    for k in range(1, n_dp):
        q = lax.rem(dp + k, n_dp)
        copy = remote(
            back_send.at[q], back_recv.at[dp], bsend_sem.at[k], brecv_sem.at[k], q, core
        )
        copy.start()
        backs.append(copy)
    own_back = pltpu.make_async_copy(back_send.at[dp], back_recv.at[dp], own_sem.at[1])
    own_back.start()

    row_ids = lax.broadcasted_iota(jnp.int32, (2 * tok, half), 0)
    col_ids = lax.broadcasted_iota(jnp.int32, (2 * tok, half), 1)
    pick = jnp.zeros((2 * tok, half), f32)
    share_rows = lax.broadcasted_iota(jnp.int32, (tok, 1), 0)
    share_units = jnp.zeros((tok, 1), jnp.int32)
    for t in range(tok):
        share_units = jnp.where(share_rows == t, first_ref[t], share_units)
        for j in range(2):
            chosen = (row_ids == j * tok + t) & (col_ids == slots[t][j])
            pick = jnp.where(chosen, 1.0, pick)
    pick = pick.astype(bf16)
    share_first = share_units.astype(f32) / 1024.0
    share_second = (1024 - share_units).astype(f32) / 1024.0

    for copy in backs:
        copy.wait()
    own_back.wait()

    got = back_recv[...].astype(f32)
    got_out = got[:, 0].reshape(half, width).astype(bf16)
    got_grad = got[:, 1].reshape(half, width).astype(bf16)
    outs = lax.dot_general(pick, got_out, NN, preferred_element_type=f32)
    grads = lax.dot_general(pick, got_grad, NN, preferred_element_type=f32)
    out_first, out_second = outs[:tok], outs[tok:]
    mixed_ref[...] = (share_first * out_first + share_second * out_second).astype(bf16)
    grad_ref[...] = (share_first * grads[:tok] + share_second * grads[tok:]).astype(bf16)
    cot = dy_ref[...].astype(f32)
    score_first = jnp.sum(cot * out_first, axis=1, keepdims=True)
    score_second = jnp.sum(cot * out_second, axis=1, keepdims=True)
    column = lax.broadcasted_iota(jnp.int32, (tok, 2), 1)
    score_ref[...] = jnp.where(column == 0, score_first, score_second)


def fused(n_dp, tokens, cotangent, routing, gate_first, gate_weight, up_weight, down_weight):
    tok, width = tokens.shape
    cap = tok // 2
    half = n_dp * cap
    hidden = down_weight.shape[0]
    f32, bf16 = jnp.float32, jnp.bfloat16
    depth = min(DEPTH, hidden // BLOCK)
    vmem = pl.BlockSpec(memory_space=pltpu.VMEM)
    smem = pl.BlockSpec(memory_space=pltpu.SMEM)
    hbm = pl.BlockSpec(memory_space=pl.ANY)
    dma = pltpu.SemaphoreType.DMA
    return pl.pallas_call(
        functools.partial(layer_kernel, n_dp),
        out_shape=(
            jax.ShapeDtypeStruct((tok, width), bf16),
            jax.ShapeDtypeStruct((tok, width), bf16),
            jax.ShapeDtypeStruct((tok, 2), f32),
        ),
        in_specs=[smem, smem, vmem, vmem, hbm, hbm, hbm],
        out_specs=(vmem, vmem, vmem),
        scratch_shapes=[
            pltpu.VMEM((depth, width, BLOCK), bf16),
            pltpu.VMEM((depth, width, BLOCK), bf16),
            pltpu.VMEM((depth, BLOCK, width), bf16),
            pltpu.VMEM((2, n_dp, cap, width), bf16),
            pltpu.VMEM((2, 2 * n_dp, cap, width), bf16),
            pltpu.VMEM((2 * half, width), bf16),
            pltpu.VMEM((2 * half, width), bf16),
            pltpu.VMEM((2 * half, width), f32),
            pltpu.VMEM((2 * half, width), f32),
            pltpu.VMEM((2, half, width), bf16),
            pltpu.VMEM((2, half, width), bf16),
            pltpu.VMEM((n_dp, 2, cap, width), bf16),
            pltpu.VMEM((n_dp, 2, cap, width), bf16),
            dma((3, depth)),
            dma((n_dp,)),
            dma((n_dp,)),
            dma((n_dp,)),
            dma((n_dp,)),
            dma((2,)),
            dma((2,)),
            dma((n_dp,)),
            dma((n_dp,)),
        ],
        compiler_params=pltpu.CompilerParams(
            collective_id=0, has_side_effects=True, vmem_limit_bytes=60 * 1024 * 1024
        ),
    )(routing, gate_first, tokens, cotangent, gate_weight, up_weight, down_weight)


def solution(mesh):
    placed = (
        P(("groups", "dp", "expert"), None),
        P(("groups", "dp", "expert"), None),
        P(("groups", "dp", "expert"), None),
        P(("groups", "dp", "expert")),
        P(None, ("dp", "expert")),
        P(None, ("dp", "expert")),
        P(("dp", "expert"), None),
    )
    n_dp = mesh.shape["dp"]
    one_chip = n_dp == E and mesh.shape["expert"] == 2
    return jax.shard_map(
        functools.partial(fused, n_dp) if one_chip else on_device,
        mesh=mesh,
        in_specs=placed,
        out_specs=(
            P(("groups", "dp", "expert"), None),
            P(("groups", "dp", "expert"), None),
            P(("groups", "dp", "expert"), None),
        ),
        check_vma=False,
    )
```

```python
import functools

import jax
import jax.numpy as jnp
from jax import lax
from jax.experimental import pallas as pl
from jax.experimental.pallas import tpu as pltpu
from jax.sharding import PartitionSpec as P

E = 8
BLOCK = 512
DEPTH = 4
NN = (((1,), (0,)), ((), ()))
NT = (((1,), (1,)), ((), ()))


def expert_rows(got_x, got_dy, got_w, gate_weight, up_weight, down_weight):
    gate_pre = jnp.dot(got_x, gate_weight, preferred_element_type=jnp.float32)
    up_pre = jnp.dot(got_x, up_weight, preferred_element_type=jnp.float32)
    sig_gate = jax.nn.sigmoid(gate_pre)
    silu_gate = gate_pre * sig_gate
    hidden = (silu_gate * up_pre).astype(jnp.bfloat16)
    part_out = jnp.dot(hidden, down_weight, preferred_element_type=jnp.float32)
    d_hidden = got_w[:, None] * jnp.dot(got_dy, down_weight.T, preferred_element_type=jnp.float32)
    d_gate = (d_hidden * up_pre * sig_gate * (1.0 + gate_pre * (1.0 - sig_gate))).astype(
        jnp.bfloat16
    )
    d_up = (d_hidden * silu_gate).astype(jnp.bfloat16)
    part_grad = jnp.dot(d_gate, gate_weight.T, preferred_element_type=jnp.float32)
    part_grad = part_grad + jnp.dot(d_up, up_weight.T, preferred_element_type=jnp.float32)
    return (part_out.astype(jnp.bfloat16), part_grad.astype(jnp.bfloat16))


def on_device(tokens, cotangent, routing, gate_first, gate_weight, up_weight, down_weight):
    devices = lax.axis_size(("dp", "expert"))
    group_size = devices // E
    tok_rows = tokens.shape[0]
    width = tokens.shape[1]
    capacity = tok_rows // 2
    expert_ids = jnp.arange(E, dtype=jnp.int32)
    first_hot = (routing[:, 0:1] == expert_ids[None, :]).astype(jnp.int32)
    second_hot = (routing[:, 1:2] == expert_ids[None, :]).astype(jnp.int32)
    rank_rows = jnp.cumsum(first_hot + second_hot, axis=0) - 1
    slot_ids = jnp.arange(capacity, dtype=jnp.int32)
    slot_hot = (rank_rows[:, :, None] == slot_ids[None, None, :]).astype(jnp.float32)
    pick_first = first_hot[:, :, None].astype(jnp.float32) * slot_hot
    pick_second = second_hot[:, :, None].astype(jnp.float32) * slot_hot
    picked = pick_first + pick_second
    share_first = gate_first.astype(jnp.float32) / 1024.0
    share_second = (1024 - gate_first).astype(jnp.float32) / 1024.0
    picked_low = picked.astype(jnp.bfloat16)
    send_x = jnp.einsum(
        "tec,td->ecd", picked_low, tokens, preferred_element_type=jnp.float32
    ).astype(jnp.bfloat16)
    send_dy = jnp.einsum(
        "tec,td->ecd", picked_low, cotangent, preferred_element_type=jnp.float32
    ).astype(jnp.bfloat16)
    weighted = pick_first * share_first[:, None, None] + pick_second * share_second[:, None, None]
    send_w = jnp.sum(weighted, axis=0)
    out_x = jnp.repeat(send_x, group_size, axis=0)
    out_dy = jnp.repeat(send_dy, group_size, axis=0)
    out_w = jnp.repeat(send_w, group_size, axis=0)

    def exchange(value):
        return lax.all_to_all(value, ("dp", "expert"), split_axis=0, concat_axis=0, tiled=True)

    recv_x, recv_dy = exchange(out_x), exchange(out_dy)
    recv_w = exchange(out_w.astype(jnp.bfloat16)).astype(out_w.dtype)
    got_x = recv_x.reshape(devices * capacity, width)
    got_dy = recv_dy.reshape(devices * capacity, width)
    got_w = recv_w.reshape(devices * capacity)
    part_out, part_grad = expert_rows(got_x, got_dy, got_w, gate_weight, up_weight, down_weight)
    back_out = exchange(part_out.reshape(devices, capacity, width))
    back_grad = exchange(part_grad.reshape(devices, capacity, width))
    summed_out = jnp.sum(
        back_out.astype(jnp.float32).reshape(E, group_size, capacity, width), axis=1
    )
    summed_grad = jnp.sum(
        back_grad.astype(jnp.float32).reshape(E, group_size, capacity, width), axis=1
    )
    rank_first = jnp.take_along_axis(rank_rows, routing[:, 0:1], axis=1)[:, 0]
    rank_second = jnp.take_along_axis(rank_rows, routing[:, 1:2], axis=1)[:, 0]
    slot_first = routing[:, 0] * capacity + rank_first
    slot_second = routing[:, 1] * capacity + rank_second
    flat_out = summed_out.reshape(E * capacity, width)
    flat_grad = summed_grad.reshape(E * capacity, width)
    out_first = jnp.take(flat_out, slot_first, axis=0)
    out_second = jnp.take(flat_out, slot_second, axis=0)
    mixed = (share_first[:, None] * out_first + share_second[:, None] * out_second).astype(
        jnp.bfloat16
    )
    token_grad = (
        jnp.take(flat_grad, slot_first, axis=0) + jnp.take(flat_grad, slot_second, axis=0)
    ).astype(jnp.bfloat16)
    cot_float = cotangent.astype(jnp.float32)
    grad_first = jnp.sum(cot_float * out_first, axis=1)
    grad_second = jnp.sum(cot_float * out_second, axis=1)
    gate_grad = jnp.stack([grad_first, grad_second], axis=1)
    return (mixed, token_grad, gate_grad)


def layer_kernel(
    n_dp,
    route_ref,
    first_ref,
    x_ref,
    dy_ref,
    gate_hbm,
    up_hbm,
    down_hbm,
    mixed_ref,
    grad_ref,
    score_ref,
    wide_buf,
    down_buf,
    acts,
    pack,
    recv,
    xs,
    dys,
    acc_out,
    acc_grad,
    pair_send,
    pair_recv,
    back_send,
    back_recv,
    w_sem,
    send_sem,
    recv_sem,
    fsend_sem,
    frecv_sem,
    own_sem,
    pair_sem,
    bsend_sem,
    brecv_sem,
):
    tok, width = x_ref.shape
    cap = tok // 2
    half = n_dp * cap
    hidden = down_hbm.shape[0]
    blocks = hidden // BLOCK
    dp = lax.axis_index("dp")
    core = lax.axis_index("expert")
    other = 1 - core
    f32, bf16 = jnp.float32, jnp.bfloat16

    def weight_copies(step, slot):
        start = pl.multiple_of(step * BLOCK, BLOCK)
        return (
            pltpu.make_async_copy(
                gate_hbm.at[:, pl.ds(start, BLOCK)],
                wide_buf.at[slot, :, pl.ds(0, BLOCK)],
                w_sem.at[0, slot],
            ),
            pltpu.make_async_copy(
                up_hbm.at[:, pl.ds(start, BLOCK)],
                wide_buf.at[slot, :, pl.ds(BLOCK, BLOCK)],
                w_sem.at[1, slot],
            ),
            pltpu.make_async_copy(
                down_hbm.at[pl.ds(start, BLOCK), :], down_buf.at[slot], w_sem.at[2, slot]
            ),
        )

    def remote(src, dst, send, arrive, q, c):
        return pltpu.make_async_remote_copy(
            src_ref=src,
            dst_ref=dst,
            send_sem=send,
            recv_sem=arrive,
            device_id={"dp": q, "expert": c},
            device_id_type=pl.DeviceIdType.MESH,
        )

    barrier = pltpu.get_barrier_semaphore()
    for k in range(1, n_dp):
        pl.semaphore_signal(
            barrier,
            inc=1,
            device_id={"dp": lax.rem(dp + k, n_dp), "expert": core},
            device_id_type=pl.DeviceIdType.MESH,
        )
    pl.semaphore_signal(
        barrier,
        inc=1,
        device_id={"dp": dp, "expert": other},
        device_id_type=pl.DeviceIdType.MESH,
    )

    ahead = min(DEPTH, blocks)
    for step in range(ahead):
        for copy in weight_copies(step, step):
            copy.start()

    slots = []
    for t in range(tok):
        row = []
        for j in range(2):
            e = route_ref[t, j]
            rank = jnp.int32(0)
            for s in range(t):
                rank = rank + jnp.where((route_ref[s, 0] == e) | (route_ref[s, 1] == e), 1, 0)
            row.append(e * cap + rank)
        slots.append(row)

    slot_rows = lax.broadcasted_iota(jnp.int32, (half, width), 0)
    for which, ref in ((0, x_ref), (1, dy_ref)):
        rows = ref[...].astype(f32)
        packed = jnp.zeros((half, width), f32)
        for t in range(tok):
            chosen = (slot_rows == slots[t][0]) | (slot_rows == slots[t][1])
            packed = jnp.where(chosen, jnp.broadcast_to(rows[t : t + 1, :], (half, width)), packed)
        for e in range(n_dp):
            pack[which, e] = packed[e * cap : (e + 1) * cap, :].astype(bf16)

    pl.semaphore_wait(barrier, n_dp)

    mine = core * n_dp + dp
    sends = []
    for k in range(1, n_dp):
        q = lax.rem(dp + k, n_dp)
        copy = remote(
            pack.at[:, q], recv.at[:, mine], send_sem.at[k], recv_sem.at[k], q, core
        )
        copy.start()
        sends.append(copy)
    own = pltpu.make_async_copy(pack.at[:, dp], recv.at[:, mine], own_sem.at[0])
    own.start()
    forwards = [
        remote(pack.at[:, dp], recv.at[:, mine], fsend_sem.at[0], frecv_sem.at[0], dp, other)
    ]
    forwards[0].start()
    for k in range(1, n_dp):
        slot = core * n_dp + lax.rem(dp + n_dp - k, n_dp)
        sends[k - 1].wait_recv()
        copy = remote(
            recv.at[:, slot], recv.at[:, slot], fsend_sem.at[k], frecv_sem.at[k], dp, other
        )
        copy.start()
        forwards.append(copy)
    own.wait()
    for copy in forwards:
        copy.wait_recv()

    xs[...] = recv[0].astype(f32).reshape(2 * half, width).astype(bf16)
    dys[...] = recv[1].astype(f32).reshape(2 * half, width).astype(bf16)
    acc_out[...] = jnp.zeros_like(acc_out)
    acc_grad[...] = jnp.zeros_like(acc_grad)

    def inner(step):
        slot = lax.rem(step, ahead)
        for copy in weight_copies(step, slot):
            copy.wait()
        pre = lax.dot_general(xs[...], wide_buf[slot], NN, preferred_element_type=f32)
        d_hidden = lax.dot_general(
            down_buf[slot], dys[...], NT, preferred_element_type=f32
        ).T
        gate_pre, up_pre = pre[:, :BLOCK], pre[:, BLOCK:]
        sig = 1.0 / (1.0 + jnp.exp(-gate_pre))
        silu = gate_pre * sig
        hid = (silu * up_pre).astype(bf16)
        d_gate = (d_hidden * up_pre * sig * (1.0 + gate_pre * (1.0 - sig))).astype(bf16)
        d_up = (d_hidden * silu).astype(bf16)
        return hid, d_gate, d_up

    def keep_acts(values):
        for n, value in enumerate(values):
            acts[:, n * BLOCK : (n + 1) * BLOCK] = value

    def add_out(hid, slot):
        acc_out[...] += lax.dot_general(hid, down_buf[slot], NN, preferred_element_type=f32)

    def add_grad(d_both, slot):
        acc_grad[...] += lax.dot_general(d_both, wide_buf[slot], NT, preferred_element_type=f32)

    keep_acts(inner(0))

    @pl.loop(1, blocks)
    def _(step):
        last = lax.rem(step - 1, ahead)
        hid, d_both = acts[:, :BLOCK], acts[:, BLOCK:]
        values = inner(step)
        add_out(hid, last)
        add_grad(d_both, last)
        keep_acts(values)

        @pl.when(step - 1 + ahead < blocks)
        def _():
            for copy in weight_copies(step - 1 + ahead, last):
                copy.start()

    keep = pl.ds(pl.multiple_of(core * half, half), half)
    give = pl.ds(pl.multiple_of(other * half, half), half)

    def to_pair(which, acc):
        pair_send[which] = acc[give, :].astype(bf16)
        copy = remote(
            pair_send.at[which],
            pair_recv.at[which],
            pair_sem.at[0, which],
            pair_sem.at[1, which],
            dp,
            other,
        )
        copy.start()
        return copy

    def to_home(which, acc):
        total = acc[keep, :] + pair_recv[which].astype(f32)
        for q in range(n_dp):
            back_send[which, q] = total[q * cap : (q + 1) * cap, :].astype(bf16)
        copies = []
        for k in range(1, n_dp):
            q = lax.rem(dp + k, n_dp)
            copy = remote(
                back_send.at[which, q],
                back_recv.at[which, dp],
                bsend_sem.at[which, k],
                brecv_sem.at[which, k],
                q,
                core,
            )
            copy.start()
            copies.append(copy)
        copy = pltpu.make_async_copy(
            back_send.at[which, dp], back_recv.at[which, dp], own_sem.at[1 + which]
        )
        copy.start()
        copies.append(copy)
        return copies

    final = (blocks - 1) % ahead
    add_out(acts[:, :BLOCK], final)
    pair_out = to_pair(0, acc_out)
    add_grad(acts[:, BLOCK:], final)
    pair_grad = to_pair(1, acc_grad)
    pair_out.wait()
    backs_out = to_home(0, acc_out)
    pair_grad.wait()
    backs_grad = to_home(1, acc_grad)
    for copy in sends:
        copy.wait_send()
    for copy in forwards:
        copy.wait_send()

    row_ids = lax.broadcasted_iota(jnp.int32, (2 * tok, half), 0)
    col_ids = lax.broadcasted_iota(jnp.int32, (2 * tok, half), 1)
    pick = jnp.zeros((2 * tok, half), f32)
    share_rows = lax.broadcasted_iota(jnp.int32, (tok, 1), 0)
    share_units = jnp.zeros((tok, 1), jnp.int32)
    for t in range(tok):
        share_units = jnp.where(share_rows == t, first_ref[t], share_units)
        for j in range(2):
            chosen = (row_ids == j * tok + t) & (col_ids == slots[t][j])
            pick = jnp.where(chosen, 1.0, pick)
    pick = pick.astype(bf16)
    share_first = share_units.astype(f32) / 1024.0
    share_second = (1024 - share_units).astype(f32) / 1024.0

    for copy in backs_out:
        copy.wait()
    got_out = back_recv[0].astype(f32).reshape(half, width).astype(bf16)
    outs = lax.dot_general(pick, got_out, NN, preferred_element_type=f32)
    out_first, out_second = outs[:tok], outs[tok:]
    mixed_ref[...] = (share_first * out_first + share_second * out_second).astype(bf16)
    cot = dy_ref[...].astype(f32)
    score_first = jnp.sum(cot * out_first, axis=1, keepdims=True)
    score_second = jnp.sum(cot * out_second, axis=1, keepdims=True)
    column = lax.broadcasted_iota(jnp.int32, (tok, 2), 1)
    score_ref[...] = jnp.where(column == 0, score_first, score_second)

    for copy in backs_grad:
        copy.wait()
    got_grad = back_recv[1].astype(f32).reshape(half, width).astype(bf16)
    grads = lax.dot_general(pick, got_grad, NN, preferred_element_type=f32)
    grad_ref[...] = (share_first * grads[:tok] + share_second * grads[tok:]).astype(bf16)


def fused(n_dp, tokens, cotangent, routing, gate_first, gate_weight, up_weight, down_weight):
    tok, width = tokens.shape
    cap = tok // 2
    half = n_dp * cap
    hidden = down_weight.shape[0]
    f32, bf16 = jnp.float32, jnp.bfloat16
    depth = min(DEPTH, hidden // BLOCK)
    vmem = pl.BlockSpec(memory_space=pltpu.VMEM)
    smem = pl.BlockSpec(memory_space=pltpu.SMEM)
    hbm = pl.BlockSpec(memory_space=pl.ANY)
    dma = pltpu.SemaphoreType.DMA
    return pl.pallas_call(
        functools.partial(layer_kernel, n_dp),
        out_shape=(
            jax.ShapeDtypeStruct((tok, width), bf16),
            jax.ShapeDtypeStruct((tok, width), bf16),
            jax.ShapeDtypeStruct((tok, 2), f32),
        ),
        in_specs=[smem, smem, vmem, vmem, hbm, hbm, hbm],
        out_specs=(vmem, vmem, vmem),
        scratch_shapes=[
            pltpu.VMEM((depth, width, 2 * BLOCK), bf16),
            pltpu.VMEM((depth, BLOCK, width), bf16),
            pltpu.VMEM((2 * half, 3 * BLOCK), bf16),
            pltpu.VMEM((2, n_dp, cap, width), bf16),
            pltpu.VMEM((2, 2 * n_dp, cap, width), bf16),
            pltpu.VMEM((2 * half, width), bf16),
            pltpu.VMEM((2 * half, width), bf16),
            pltpu.VMEM((2 * half, width), f32),
            pltpu.VMEM((2 * half, width), f32),
            pltpu.VMEM((2, half, width), bf16),
            pltpu.VMEM((2, half, width), bf16),
            pltpu.VMEM((2, n_dp, cap, width), bf16),
            pltpu.VMEM((2, n_dp, cap, width), bf16),
            dma((3, depth)),
            dma((n_dp,)),
            dma((n_dp,)),
            dma((n_dp,)),
            dma((n_dp,)),
            dma((3,)),
            dma((2, 2)),
            dma((2, n_dp)),
            dma((2, n_dp)),
        ],
        compiler_params=pltpu.CompilerParams(
            collective_id=0, has_side_effects=True, vmem_limit_bytes=60 * 1024 * 1024
        ),
    )(routing, gate_first, tokens, cotangent, gate_weight, up_weight, down_weight)


def solution(mesh):
    placed = (
        P(("groups", "dp", "expert"), None),
        P(("groups", "dp", "expert"), None),
        P(("groups", "dp", "expert"), None),
        P(("groups", "dp", "expert")),
        P(None, ("dp", "expert")),
        P(None, ("dp", "expert")),
        P(("dp", "expert"), None),
    )
    n_dp = mesh.shape["dp"]
    one_chip = n_dp == E and mesh.shape["expert"] == 2
    return jax.shard_map(
        functools.partial(fused, n_dp) if one_chip else on_device,
        mesh=mesh,
        in_specs=placed,
        out_specs=(
            P(("groups", "dp", "expert"), None),
            P(("groups", "dp", "expert"), None),
            P(("groups", "dp", "expert"), None),
        ),
        check_vma=False,
    )
```
